1024 devices in a mesh: row: 16 (over y, core), col: 16 (over z), layer: 4 (over x).
Axes of the slice: x: 4, y: 8, z: 16, core: 2. Of those that a mesh axis runs over, the one named last changes fastest.
Arguments:
- a_panel: bfloat16 [8, 8192, 1024], P('layer', 'row', 'col'), may hold values from -6 to 6
- b_panel: bfloat16 [8, 1024, 16384], P('layer', 'row', 'col'), may hold values from -0.1875 to 0.1875
- a_mask: int32 [8, 128, 16], P('layer', 'row', 'col'), may hold values from 0 to 1, as said below
- b_mask: int32 [8, 16, 256], P('layer', 'row', 'col'), may hold values from 0 to 1, as said below
- c_pattern: int32 [128, 256], P(('row', 'layer'), 'col'), may hold values from 0 to 1, as said below
Outputs:
- filtered: float32 [8192, 16384], P(('row', 'layer'), 'col')
The draws below stay inside these ranges and needn't reach their ends.
Inputs may be any that keep to these rules, and one draw needn't show every extreme that they name: `a_mask`: 1 marks a nonzero block; in every step, every block column and every aligned group of 8 block rows holds at most 2 ones, and some such group holds exactly 2. `b_mask`: 1 marks a nonzero block; in every step, every block row and every aligned group of 16 block columns holds at most 4 ones, and some such group holds exactly 4. `c_pattern`: 1 marks a kept block.
All inputs are finite; a program needn't handle non-finite values.
Results may differ from the reference program's by a relative error of at most 0.0003.
Values may be sent and summed in bfloat16 or wider, within the bound.
No kernel may reach another device: no remote copies, remote signals or barrier semaphores. Data moves between devices by JAX's collectives and lax.ppermute only.
A program may use at most 64 MiB of HBM per device.

```python
import jax
import jax.numpy as jnp
from jax import lax

BS = 64
BR = 8
BC = 16
KB = 16
MOSTA = 2
MOSTB = 4
LSTEPS = 8
KW = 1024
ROWS = 8192
COLS = 16384
BROWS = 128
BCOLS = 256


def level_mask(key, lead, first, second, by_first):
    noise = jax.random.randint(jax.random.fold_in(key, 11), (lead, first, second), 0, 1000)
    count = first if by_first else second
    levels = jax.random.randint(jax.random.fold_in(key, 23), (count,), 0, 8)
    limits = 250 + 100 * levels
    if by_first:
        bound = limits[None, :, None]
    else:
        bound = limits[None, None, :]
    return (noise < bound).astype(jnp.int32)


def bounded_mask(key, lead, total, group, other, most):
    groups = total // group
    counts = jax.random.randint(jax.random.fold_in(key, 31), (lead * groups * other,), 0, most + 1)
    place = jax.random.randint(jax.random.fold_in(key, 37), (), 0, lead * groups * other)
    counts = counts.at[place].set(most).reshape(lead, groups, 1, other)
    levels = jax.random.randint(jax.random.fold_in(key, 41), (total,), 0, 4)
    noise = jax.random.randint(jax.random.fold_in(key, 43), (lead, total, other), 0, 1000)
    inside = jnp.arange(total, dtype=jnp.int32) % group
    priority = (noise + 700 * levels[None, :, None]) * group + inside[None, :, None]
    priority = priority.reshape(lead, groups, group, other)
    higher = jnp.sum((priority[:, :, None, :, :] > priority[:, :, :, None, :]).astype(jnp.int32), axis=3)
    ones = (higher < counts).astype(jnp.int32)
    return ones.reshape(lead, total, other)


def draw_a_mask(key, part):
    return bounded_mask(jax.random.fold_in(key, 101), LSTEPS, BROWS, BR, KB, MOSTA)


def draw_b_mask(key, part):
    drawn = bounded_mask(jax.random.fold_in(key, 202), LSTEPS, BCOLS, BC, KB, MOSTB)
    return jnp.swapaxes(drawn, 1, 2)


def draw_c_pattern(key, part):
    return level_mask(jax.random.fold_in(key, 303), 1, BROWS, BCOLS, True)[0]


def shard_levels(own_key, dims, pieces, smallest, top_value):
    level = 1.0
    for position, shards_of in pieces:
        draws = jax.random.uniform(jax.random.fold_in(jax.random.fold_in(own_key, 6), position), (shards_of,), jnp.float32, smallest / len(pieces), top_value / len(pieces))
        level = level * jnp.repeat(jnp.exp(draws), dims[position] // shards_of).reshape((-1,) + (1,) * (len(dims) - 1 - position))
    return level


def normal_values(own_key, extent, scale, most, pieces=(), kind=jnp.bfloat16):
    result = jax.random.normal(own_key, extent, jnp.float32) * scale
    if len(pieces) > 0:
        result = shard_levels(own_key, extent, pieces, -0.22, 0.18) * result
    return jnp.clip(result, min=-most, max=most).astype(kind)


def setup_inputs(seed: int = 0) -> dict:
    keys = jax.random.split(jax.random.key(seed), 6)
    return {
        "a_panel": normal_values(keys[0], (LSTEPS, ROWS, KW), 1.0, 6.0, ((0, 4), (1, 16), (2, 16))),
        "b_panel": normal_values(keys[1], (LSTEPS, KW, COLS), KW ** -0.5, 0.1875, ((0, 4), (1, 16), (2, 16))),
        "a_mask": draw_a_mask(jax.random.fold_in(keys[5], 71), 0),
        "b_mask": draw_b_mask(jax.random.fold_in(keys[5], 71), 0),
        "c_pattern": draw_c_pattern(jax.random.fold_in(keys[5], 71), 0),
    }


def spread(mask, width):
    lead = mask.shape[:-2]
    first, second = mask.shape[-2], mask.shape[-1]
    grown = jnp.broadcast_to(mask[..., :, None, :, None], lead + (first, width, second, width))
    return grown.reshape(lead + (first * width, second * width))


def reference(a_panel, b_panel, a_mask, b_mask, c_pattern):
    a_live = a_panel * spread(a_mask.astype(jnp.bfloat16), BS)
    b_live = b_panel * spread(b_mask.astype(jnp.bfloat16), BS)

    def advance(total, pair):
        left, right = pair
        return total + jnp.dot(left, right, preferred_element_type=jnp.float32), None

    start = jnp.zeros((a_live.shape[1], b_live.shape[2]), jnp.float32)
    product, _ = lax.scan(advance, start, (a_live, b_live))
    return product * spread(c_pattern.astype(jnp.float32), BS)
```

```python
import functools

import jax
import jax.numpy as jnp
from jax import lax
from jax.experimental import pallas as pl
from jax.experimental.pallas import tpu as pltpu
from jax.sharding import PartitionSpec as P

BS = 64
BR = 8
BC = 16
KB = 16
MOSTA = 2
MOSTB = 4
STEPS = 2
LAYERS = 4
NONE = 100
EXTRA = 8

F32, BF16, I32, I16 = jnp.float32, jnp.bfloat16, jnp.int32, jnp.int16
SMEM = pl.BlockSpec(memory_space=pltpu.SMEM)
VMEM = pl.BlockSpec(memory_space=pltpu.VMEM)


def grant(mib):
    return pltpu.CompilerParams(vmem_limit_bytes=mib * 2**20)


def lanes(rows=1):
    return lax.broadcasted_iota(I32, (rows, 128), 1)


def halves(left, right, rows=1):
    return jnp.where(lanes(rows) < BS, left, right)


def slot_ids(bits, most):
    ids = [jnp.int32(NONE)] * most
    seen = jnp.int32(0)
    for i, bit in enumerate(bits):
        one = bit != 0
        for s in range(most):
            ids[s] = jnp.where(one & (seen == s), jnp.int32(i), ids[s])
        seen = seen + one.astype(I32)
    return ids


def swap_halves(x):
    return pltpu.roll(x, BS, 1)


def compact(panel, pairs, ids):
    outs = [jnp.zeros((BS, 128), F32) for _ in range(len(ids) // 2)]
    for p in range(pairs):
        straight = panel(p)
        turned = swap_halves(straight)
        for o in range(len(outs)):
            want = halves(ids[2 * o], ids[2 * o + 1], BS)
            outs[o] = jnp.where(want == halves(2 * p, 2 * p + 1, BS), straight, outs[o])
            outs[o] = jnp.where(want == halves(2 * p + 1, 2 * p, BS), turned, outs[o])
    return outs


def pack_a_kernel(mask, at, out):
    ids = [slot_ids([mask[s, i] for i in range(BR)], MOSTA) for s in range(STEPS)]
    steps = [
        compact(lambda p: at[s, :, 128 * p : 128 * p + 128].astype(F32), BR // 2, ids[s])[0]
        for s in range(STEPS)
    ]
    body = jnp.concatenate(steps, axis=0).T.astype(BF16)
    row = lax.broadcasted_iota(I32, (EXTRA, 128), 0)
    index = jnp.where(
        row == 0,
        halves(ids[0][0], ids[1][0], EXTRA),
        halves(ids[0][1], ids[1][1], EXTRA),
    )
    index = index.astype(F32).astype(BF16)
    for d in range(out.shape[0]):
        out[d, 0:128, :] = body
        out[d, 128 : 128 + EXTRA, :] = index


def pack_b_kernel(mask, b, out):
    row = lax.broadcasted_iota(I32, (EXTRA, 128), 0)
    ids = [slot_ids([mask[s, j] for j in range(BC)], MOSTB) for s in range(STEPS)]
    for s in range(STEPS):
        pair = compact(lambda p: b[s, :, 128 * p : 128 * p + 128].astype(F32), BC // 2, ids[s])
        for o in range(2):
            out[BS * s : BS * s + BS, 128 * o : 128 * o + 128] = pair[o].astype(BF16)
    for o in range(2):
        index = jnp.where(
            row == 0,
            halves(ids[0][2 * o], ids[0][2 * o + 1], EXTRA),
            halves(ids[1][2 * o], ids[1][2 * o + 1], EXTRA),
        )
        out[128 : 128 + EXTRA, 128 * o : 128 * o + 128] = index.astype(F32).astype(BF16)


def spread_b_kernel(core, own, other, out):
    odd = core[0]

    def chunk(source, y, place):
        index = source[y, 128 : 128 + EXTRA, :].astype(F32)
        parts = []
        for o in range(2):
            straight = index[:, 128 * o : 128 * o + 128]
            parts += [straight, swap_halves(straight)]
        for s in range(STEPS):
            data = []
            for o in range(2):
                half = source[y, BS * s : BS * s + BS, 128 * o : 128 * o + 128]
                data += [half, swap_halves(half.astype(F32)).astype(BF16)]
            for p in range(BC // 2):
                target = halves(2 * p, 2 * p + 1, EXTRA).astype(F32)
                total = None
                for part, values in zip(parts, data):
                    chosen = jnp.where(part == target, 1.0, 0.0)[s : s + 1].astype(BF16)
                    term = values * chosen
                    total = term if total is None else total + term
                out[place, BS * s : BS * s + BS, 128 * p : 128 * p + 128] = total

    def step(y, carry):
        chunk(own, y, 2 * y + odd)
        chunk(other, y, 2 * y + 1 - odd)
        return carry

    lax.fori_loop(0, own.shape[0], step, 0)


def product_kernel(a, b, out, dense):
    @pl.when(pl.program_id(0) == 0)
    def _():
        for c in range(KB):
            index = a[c, 128 : 128 + EXTRA, :].astype(F32)
            for i in range(BR):
                total = None
                for s in range(MOSTA):
                    chosen = jnp.where(index == float(i), 1.0, 0.0)[s : s + 1].astype(BF16)
                    term = a[c, BS * s : BS * s + BS, :] * chosen
                    total = term if total is None else total + term
                dense[BS * i : BS * i + BS, 128 * c : 128 * c + 128] = total

    width = out.shape[2]
    rows = out.shape[1] - EXTRA
    right = b[...].reshape(KB * 128, width)
    total = jnp.dot(dense[...], right, preferred_element_type=F32)
    for l in range(LAYERS):
        part = total[rows * l : rows * l + rows]
        top = jnp.max(jnp.abs(part), axis=0, keepdims=True)
        power = jnp.floor(jnp.log2(jnp.maximum(top, 1e-30))) - 13.0
        out[l, 0:rows, :] = jnp.round(part * jnp.exp2(-power)).astype(I32).astype(I16)
        out[l, rows : rows + EXTRA, :] = jnp.broadcast_to(power, (EXTRA, width)).astype(I32).astype(I16)


def filter_kernel(parts, keep, out):
    rows = out.shape[0]
    total = None
    for l in range(LAYERS):
        power = parts[l, rows : rows + EXTRA, :].astype(I32).astype(F32)[0:1]
        term = parts[l, 0:rows, :].astype(I32).astype(F32) * jnp.exp2(power)
        total = term if total is None else total + term
    for i in range(rows // BS):
        out[BS * i : BS * i + BS, :] = total[BS * i : BS * i + BS] * keep[i : i + 1, :]


def body(a_panel, b_panel, a_mask, b_mask, c_pattern):
    core = lax.rem(lax.axis_index("row"), 2).astype(I32).reshape(1)
    a_sent = pl.pallas_call(
        pack_a_kernel,
        out_shape=jax.ShapeDtypeStruct((KB, 128 + EXTRA, 128), BF16),
        in_specs=[SMEM, VMEM],
        out_specs=VMEM,
        cost_estimate=pl.CostEstimate(flops=10**6, bytes_accessed=10**6, transcendentals=0),
        compiler_params=grant(4),
        name="pack_a",
    )(a_mask.reshape(STEPS, BR), jnp.swapaxes(a_panel, 1, 2))
    a_all = lax.all_to_all(a_sent, "col", 0, 0, tiled=True)
    b_sent = pl.pallas_call(
        pack_b_kernel,
        out_shape=jax.ShapeDtypeStruct((128 + EXTRA, 256), BF16),
        in_specs=[SMEM, VMEM],
        out_specs=VMEM,
        cost_estimate=pl.CostEstimate(flops=10**6, bytes_accessed=10**6, transcendentals=0),
        compiler_params=grant(4),
        name="pack_b",
    )(b_mask.reshape(STEPS, BC), b_panel)
    same_core = [[2 * y + c for y in range(8)] for c in range(2)]
    b_own = lax.all_gather(b_sent, "row", axis_index_groups=same_core)
    b_other = lax.ppermute(b_own, "row", [(r, r ^ 1) for r in range(16)])
    b_dense = pl.pallas_call(
        spread_b_kernel,
        out_shape=jax.ShapeDtypeStruct((KB, 128, 1024), BF16),
        in_specs=[SMEM, VMEM, VMEM],
        out_specs=VMEM,
        cost_estimate=pl.CostEstimate(flops=10**7, bytes_accessed=6 * 10**6, transcendentals=0),
        compiler_params=grant(12),
        name="spread_b",
    )(core, b_own, b_other)
    keep = jnp.repeat(c_pattern.astype(F32), BS, axis=1)
    width = 256
    sums = pl.pallas_call(
        product_kernel,
        out_shape=jax.ShapeDtypeStruct((LAYERS, 128 + EXTRA, 1024), I16),
        grid=(1024 // width,),
        in_specs=[
            pl.BlockSpec((KB, 128 + EXTRA, 128), lambda j: (0, 0, 0)),
            pl.BlockSpec((KB, 128, width), lambda j: (0, 0, j)),
        ],
        out_specs=pl.BlockSpec((LAYERS, 128 + EXTRA, width), lambda j: (0, 0, j)),
        scratch_shapes=[pltpu.VMEM((512, KB * 128), BF16)],
        cost_estimate=pl.CostEstimate(flops=2 * 10**9, bytes_accessed=6 * 10**6, transcendentals=0),
        compiler_params=grant(16),
        name="product",
    )(a_all, b_dense)
    parts = lax.all_to_all(sums, "layer", 0, 0, tiled=True)
    return pl.pallas_call(
        filter_kernel,
        out_shape=jax.ShapeDtypeStruct((128, 1024), F32),
        in_specs=[VMEM, VMEM],
        out_specs=VMEM,
        cost_estimate=pl.CostEstimate(flops=10**6, bytes_accessed=2 * 10**6, transcendentals=0),
        compiler_params=grant(8),
        name="filter",
    )(parts, keep)


def solution(mesh):
    spec = P("layer", "row", "col")
    out = P(("row", "layer"), "col")
    return jax.shard_map(
        body, mesh=mesh, in_specs=(spec, spec, spec, spec, out), out_specs=out, check_vma=False
    )
```

```python
import functools

import jax
import jax.numpy as jnp
from jax import lax
from jax.experimental import pallas as pl
from jax.experimental.pallas import tpu as pltpu
from jax.sharding import PartitionSpec as P

BS = 64
BR = 8
BC = 16
KB = 16
MOSTA = 2
MOSTB = 4
STEPS = 2
LAYERS = 4
NONE = 100
EXTRA = 8

F32, BF16, I32, I16 = jnp.float32, jnp.bfloat16, jnp.int32, jnp.int16
ANY = pl.BlockSpec(memory_space=pl.ANY)
VMEM = pl.BlockSpec(memory_space=pltpu.VMEM)


def grant(mib):
    return pltpu.CompilerParams(vmem_limit_bytes=mib * 2**20)


def lanes(rows=1):
    return lax.broadcasted_iota(I32, (rows, 128), 1)


def halves(left, right, rows=1):
    return jnp.where(lanes(rows) < BS, left, right)


def slot_ids(bits, most):
    ids = [jnp.int32(NONE)] * most
    seen = jnp.int32(0)
    for i, bit in enumerate(bits):
        one = bit != 0
        for s in range(most):
            ids[s] = jnp.where(one & (seen == s), jnp.int32(i), ids[s])
        seen = seen + one.astype(I32)
    return ids


def swap_halves(x):
    return pltpu.roll(x, BS, 1)


def compact(panel, pairs, ids):
    outs = [jnp.zeros((BS, 128), F32) for _ in range(len(ids) // 2)]
    for p in range(pairs):
        straight = panel(p)
        turned = swap_halves(straight)
        for o in range(len(outs)):
            want = halves(ids[2 * o], ids[2 * o + 1], BS)
            outs[o] = jnp.where(want == halves(2 * p, 2 * p + 1, BS), straight, outs[o])
            outs[o] = jnp.where(want == halves(2 * p + 1, 2 * p, BS), turned, outs[o])
    return outs


def pack_kernel(a_mask, b_mask, at, b, a_out, b_out, a_bits, b_bits, a_in, b_in, a_packed, b_packed, sems):
    loads = [
        pltpu.make_async_copy(source, target, sems.at[n])
        for n, (source, target) in enumerate(((b_mask, b_bits), (b, b_in), (a_mask, a_bits), (at, a_in)))
    ]
    for load in loads:
        load.start()
    row = lax.broadcasted_iota(I32, (EXTRA, 128), 0)

    loads[0].wait()
    ids = [slot_ids([b_bits[s, j] for j in range(BC)], MOSTB) for s in range(STEPS)]
    loads[1].wait()
    for s in range(STEPS):
        pair = compact(lambda p: b_in[s, :, 128 * p : 128 * p + 128].astype(F32), BC // 2, ids[s])
        for o in range(2):
            b_packed[BS * s : BS * s + BS, 128 * o : 128 * o + 128] = pair[o].astype(BF16)
    for o in range(2):
        index = jnp.where(
            row == 0,
            halves(ids[0][2 * o], ids[0][2 * o + 1], EXTRA),
            halves(ids[1][2 * o], ids[1][2 * o + 1], EXTRA),
        )
        b_packed[128 : 128 + EXTRA, 128 * o : 128 * o + 128] = index.astype(F32).astype(BF16)
    stores = [pltpu.make_async_copy(b_packed, b_out.at[d], sems.at[5 + d]) for d in range(KB)]
    for store in stores:
        store.start()

    loads[2].wait()
    ids = [slot_ids([a_bits[s, i] for i in range(BR)], MOSTA) for s in range(STEPS)]
    loads[3].wait()
    steps = [
        compact(lambda p: a_in[s, :, 128 * p : 128 * p + 128].astype(F32), BR // 2, ids[s])[0]
        for s in range(STEPS)
    ]
    a_packed[0:128, :] = jnp.concatenate(steps, axis=0).T.astype(BF16)
    index = jnp.where(
        row == 0,
        halves(ids[0][0], ids[1][0], EXTRA),
        halves(ids[0][1], ids[1][1], EXTRA),
    )
    a_packed[128 : 128 + EXTRA, :] = index.astype(F32).astype(BF16)
    stores.append(pltpu.make_async_copy(a_packed, a_out, sems.at[4]))
    stores[-1].start()
    for store in stores:
        store.wait()


def spread_b(source, k, row, total):
    for s in range(STEPS):
        parts = []
        for o in range(2):
            index = source[k, 128 : 128 + EXTRA, 128 * o : 128 * o + 128].astype(F32)
            half = source[k, BS * s : BS * s + BS, 128 * o : 128 * o + 128]
            for ids, values in (
                (index, half),
                (swap_halves(index), swap_halves(half.astype(F32)).astype(BF16)),
            ):
                ids = jnp.broadcast_to(ids[s : s + 1], (BS, 128)).astype(BF16)
                parts.append((ids, values))
        for p in range(BC // 2):
            target = halves(2 * p, 2 * p + 1, BS).astype(F32).astype(BF16)
            dense = jnp.zeros((BS, 128), BF16)
            for ids, values in parts:
                dense = jnp.where(ids == target, values, dense)
            total[p // 2, pl.ds(row + BS * s, BS), 128 * (p % 2) : 128 * (p % 2) + 128] = dense


def product_kernel(a, b, out, left, right):
    def spread(k, carry):
        spread_b(b, k, pl.multiple_of(k * 128, 128), right)
        return carry

    lax.fori_loop(0, KB, spread, 0, unroll=2)
    for c in range(KB):
        index = a[c, 128 : 128 + EXTRA, :].astype(F32)
        ids = [jnp.broadcast_to(index[s : s + 1], (BS, 128)).astype(BF16) for s in range(MOSTA)]
        for i in range(BR):
            dense = jnp.zeros((BS, 128), BF16)
            for s in range(MOSTA):
                dense = jnp.where(ids[s] == jnp.bfloat16(i), a[c, BS * s : BS * s + BS, :], dense)
            left[BS * i : BS * i + BS, 128 * c : 128 * c + 128] = dense
    rows = out.shape[1] - EXTRA
    tiles, _, width = right.shape
    for t in range(tiles):
        cols = slice(width * t, width * t + width)
        total = jnp.dot(left[...], right[t], preferred_element_type=F32)
        for l in range(LAYERS):
            part = total[rows * l : rows * l + rows]
            top = jnp.max(jnp.abs(part), axis=0, keepdims=True)
            power = jnp.floor(jnp.log2(jnp.maximum(top, 1e-30))) - 13.0
            out[l, 0:rows, cols] = jnp.round(part * jnp.exp2(-power)).astype(I32).astype(I16)
            power = jnp.broadcast_to(power, (EXTRA, width))
            out[l, rows : rows + EXTRA, cols] = power.astype(I32).astype(I16)


def filter_kernel(parts, keep, out):
    rows = out.shape[0]
    total = None
    for l in range(LAYERS):
        power = parts[l, rows : rows + EXTRA, :].astype(I32).astype(F32)[0:1]
        term = parts[l, 0:rows, :].astype(I32).astype(F32) * jnp.exp2(power)
        total = term if total is None else total + term
    for i in range(rows // BS):
        out[BS * i : BS * i + BS, :] = total[BS * i : BS * i + BS] * keep[i : i + 1, :]


def body(a_panel, b_panel, a_mask, b_mask, c_pattern):
    rows = 128 + EXTRA
    a_sent, b_sent = pl.pallas_call(
        pack_kernel,
        out_shape=(
            jax.ShapeDtypeStruct((rows, 128), BF16),
            jax.ShapeDtypeStruct((KB, rows, 256), BF16),
        ),
        in_specs=[ANY] * 4,
        out_specs=(ANY, ANY),
        scratch_shapes=[
            pltpu.SMEM((STEPS, BR), I32),
            pltpu.SMEM((STEPS, BC), I32),
            pltpu.VMEM((STEPS, BS, BR * BS), BF16),
            pltpu.VMEM((STEPS, BS, BC * BS), BF16),
            pltpu.VMEM((rows, 128), BF16),
            pltpu.VMEM((rows, 256), BF16),
            pltpu.SemaphoreType.DMA((5 + KB,)),
        ],
        cost_estimate=pl.CostEstimate(flops=10**6, bytes_accessed=2 * 10**6, transcendentals=0),
        name="pack",
    )(
        a_mask.reshape(STEPS, BR),
        b_mask.reshape(STEPS, BC),
        jnp.swapaxes(a_panel, 1, 2),
        b_panel,
    )
    b_all = lax.all_to_all(b_sent, "row", 0, 0, tiled=True)
    a_all = lax.all_gather(a_sent, "col")
    keep = jnp.repeat(c_pattern.astype(F32), BS, axis=1)
    sums = pl.pallas_call(
        product_kernel,
        out_shape=jax.ShapeDtypeStruct((LAYERS, 128 + EXTRA, 1024), I16),
        in_specs=[VMEM, VMEM],
        out_specs=VMEM,
        scratch_shapes=[
            pltpu.VMEM((BR * BS, KB * 128), BF16),
            pltpu.VMEM((4, KB * 128, 256), BF16),
        ],
        cost_estimate=pl.CostEstimate(flops=2 * 10**9, bytes_accessed=6 * 10**6, transcendentals=0),
        compiler_params=grant(24),
        name="product",
    )(a_all, b_all)
    parts = lax.all_to_all(sums, "layer", 0, 0, tiled=True)
    return pl.pallas_call(
        filter_kernel,
        out_shape=jax.ShapeDtypeStruct((128, 1024), F32),
        in_specs=[VMEM, VMEM],
        out_specs=VMEM,
        cost_estimate=pl.CostEstimate(flops=10**6, bytes_accessed=2 * 10**6, transcendentals=0),
        compiler_params=grant(8),
        name="filter",
    )(parts, keep)


def solution(mesh):
    spec = P("layer", "row", "col")
    out = P(("row", "layer"), "col")
    return jax.shard_map(
        body, mesh=mesh, in_specs=(spec, spec, spec, spec, out), out_specs=out, check_vma=False
    )
```

```python
import functools

import jax
import jax.numpy as jnp
from jax import lax
from jax.experimental import pallas as pl
from jax.experimental.pallas import tpu as pltpu
from jax.sharding import PartitionSpec as P

BS = 64
BR = 8
BC = 16
KB = 16
MOSTA = 2
MOSTB = 4
STEPS = 2
LAYERS = 4
NONE = 100
EXTRA = 8

F32, BF16, I32, I16 = jnp.float32, jnp.bfloat16, jnp.int32, jnp.int16
ANY = pl.BlockSpec(memory_space=pl.ANY)
VMEM = pl.BlockSpec(memory_space=pltpu.VMEM)


def grant(mib):
    return pltpu.CompilerParams(vmem_limit_bytes=mib * 2**20)


def lanes(rows=1):
    return lax.broadcasted_iota(I32, (rows, 128), 1)


def halves(left, right, rows=1):
    return jnp.where(lanes(rows) < BS, left, right)


def slot_ids(bits, most):
    ids = [jnp.int32(NONE)] * most
    seen = jnp.int32(0)
    for i, bit in enumerate(bits):
        one = bit != 0
        for s in range(most):
            ids[s] = jnp.where(one & (seen == s), jnp.int32(i), ids[s])
        seen = seen + one.astype(I32)
    return ids


def swap_halves(x):
    return pltpu.roll(x, BS, 1)


def compact(panel, pairs, ids):
    outs = [jnp.zeros((BS, 128), F32) for _ in range(len(ids) // 2)]
    for p in range(pairs):
        straight = panel(p)
        turned = swap_halves(straight)
        for o in range(len(outs)):
            want = halves(ids[2 * o], ids[2 * o + 1], BS)
            outs[o] = jnp.where(want == halves(2 * p, 2 * p + 1, BS), straight, outs[o])
            outs[o] = jnp.where(want == halves(2 * p + 1, 2 * p, BS), turned, outs[o])
    return outs


def pack_kernel(a_mask, b_mask, at, b, a_out, b_out, a_bits, b_bits, a_in, b_in, a_packed, b_packed, sems):
    loads = [
        pltpu.make_async_copy(source, target, sems.at[n])
        for n, (source, target) in enumerate(((b_mask, b_bits), (b, b_in), (a_mask, a_bits), (at, a_in)))
    ]
    for load in loads:
        load.start()
    row = lax.broadcasted_iota(I32, (EXTRA, 128), 0)

    loads[0].wait()
    ids = [slot_ids([b_bits[s, j] for j in range(BC)], MOSTB) for s in range(STEPS)]
    loads[1].wait()
    for s in range(STEPS):
        pair = compact(lambda p: b_in[s, :, 128 * p : 128 * p + 128].astype(F32), BC // 2, ids[s])
        for o in range(2):
            b_packed[BS * s : BS * s + BS, 128 * o : 128 * o + 128] = pair[o].astype(BF16)
    for o in range(2):
        index = jnp.where(
            row == 0,
            halves(ids[0][2 * o], ids[0][2 * o + 1], EXTRA),
            halves(ids[1][2 * o], ids[1][2 * o + 1], EXTRA),
        )
        b_packed[128 : 128 + EXTRA, 128 * o : 128 * o + 128] = index.astype(F32).astype(BF16)
    stores = [pltpu.make_async_copy(b_packed, b_out.at[d], sems.at[5 + d]) for d in range(KB)]
    for store in stores:
        store.start()

    loads[2].wait()
    ids = [slot_ids([a_bits[s, i] for i in range(BR)], MOSTA) for s in range(STEPS)]
    loads[3].wait()
    steps = [
        compact(lambda p: a_in[s, :, 128 * p : 128 * p + 128].astype(F32), BR // 2, ids[s])[0]
        for s in range(STEPS)
    ]
    a_packed[0:128, :] = jnp.concatenate(steps, axis=0).T.astype(BF16)
    index = jnp.where(
        row == 0,
        halves(ids[0][0], ids[1][0], EXTRA),
        halves(ids[0][1], ids[1][1], EXTRA),
    )
    a_packed[128 : 128 + EXTRA, :] = index.astype(F32).astype(BF16)
    stores.append(pltpu.make_async_copy(a_packed, a_out, sems.at[4]))
    stores[-1].start()
    for store in stores:
        store.wait()


def turn(b, k, s):
    parts = []
    for o in range(2):
        index = b[k, 128 : 128 + EXTRA, 128 * o : 128 * o + 128].astype(F32)
        half = b[k, BS * s : BS * s + BS, 128 * o : 128 * o + 128]
        for ids, values in (
            (index, half),
            (swap_halves(index), swap_halves(half.astype(F32)).astype(BF16)),
        ):
            parts.append((jnp.broadcast_to(ids[s : s + 1], (BS, 128)).astype(BF16), values))
    return parts


def pick(parts, p):
    target = halves(2 * p, 2 * p + 1, BS).astype(F32).astype(BF16)
    dense = jnp.zeros((BS, 128), BF16)
    for ids, values in parts:
        dense = jnp.where(ids == target, values, dense)
    return dense


def product_kernel(a, b, out, left):
    for c in range(KB):
        index = a[c, 128 : 128 + EXTRA, :].astype(F32)
        ids = [jnp.broadcast_to(index[s : s + 1], (BS, 128)).astype(BF16) for s in range(MOSTA)]
        for i in range(BR):
            dense = jnp.zeros((BS, 128), BF16)
            for s in range(MOSTA):
                dense = jnp.where(ids[s] == jnp.bfloat16(i), a[c, BS * s : BS * s + BS, :], dense)
            left[BS * i : BS * i + BS, 128 * c : 128 * c + 128] = dense
    rows = out.shape[1] - EXTRA
    tiles, width = 1, 1024
    for t in range(tiles):
        cols = slice(width * t, width * t + width)
        dense = []
        for k in range(KB):
            for s in range(STEPS):
                parts = turn(b, k, s)
                dense.append(jnp.concatenate([pick(parts, h) for h in range(8)], axis=1))
        total = jnp.dot(left[...], jnp.concatenate(dense, axis=0), preferred_element_type=F32)
        for l in range(LAYERS):
            part = total[rows * l : rows * l + rows]
            top = jnp.max(jnp.abs(part), axis=0, keepdims=True)
            power = jnp.floor(jnp.log2(jnp.maximum(top, 1e-30))) - 13.0
            out[l, 0:rows, cols] = jnp.round(part * jnp.exp2(-power)).astype(I32).astype(I16)
            power = jnp.broadcast_to(power, (EXTRA, width))
            out[l, rows : rows + EXTRA, cols] = power.astype(I32).astype(I16)


def filter_kernel(parts, keep, out):
    rows = out.shape[0]
    total = None
    for l in range(LAYERS):
        power = parts[l, rows : rows + EXTRA, :].astype(I32).astype(F32)[0:1]
        term = parts[l, 0:rows, :].astype(I32).astype(F32) * jnp.exp2(power)
        total = term if total is None else total + term
    for i in range(rows // BS):
        out[BS * i : BS * i + BS, :] = total[BS * i : BS * i + BS] * keep[i : i + 1, :]


def body(a_panel, b_panel, a_mask, b_mask, c_pattern):
    rows = 128 + EXTRA
    a_sent, b_sent = pl.pallas_call(
        pack_kernel,
        out_shape=(
            jax.ShapeDtypeStruct((rows, 128), BF16),
            jax.ShapeDtypeStruct((KB, rows, 256), BF16),
        ),
        in_specs=[ANY] * 4,
        out_specs=(ANY, ANY),
        scratch_shapes=[
            pltpu.SMEM((STEPS, BR), I32),
            pltpu.SMEM((STEPS, BC), I32),
            pltpu.VMEM((STEPS, BS, BR * BS), BF16),
            pltpu.VMEM((STEPS, BS, BC * BS), BF16),
            pltpu.VMEM((rows, 128), BF16),
            pltpu.VMEM((rows, 256), BF16),
            pltpu.SemaphoreType.DMA((5 + KB,)),
        ],
        cost_estimate=pl.CostEstimate(flops=10**6, bytes_accessed=2 * 10**6, transcendentals=0),
        name="pack",
    )(
        a_mask.reshape(STEPS, BR),
        b_mask.reshape(STEPS, BC),
        jnp.swapaxes(a_panel, 1, 2),
        b_panel,
    )
    b_all = lax.all_to_all(b_sent, "row", 0, 0, tiled=True)
    a_all = lax.all_gather(a_sent, "col")
    keep = jnp.repeat(c_pattern.astype(F32), BS, axis=1)
    sums = pl.pallas_call(
        product_kernel,
        out_shape=jax.ShapeDtypeStruct((LAYERS, 128 + EXTRA, 1024), I16),
        in_specs=[VMEM, VMEM],
        out_specs=VMEM,
        scratch_shapes=[
            pltpu.VMEM((BR * BS, KB * 128), BF16),
        ],
        cost_estimate=pl.CostEstimate(flops=2 * 10**9, bytes_accessed=6 * 10**6, transcendentals=0),
        compiler_params=grant(24),
        name="product",
    )(a_all, b_all)
    parts = lax.all_to_all(sums, "layer", 0, 0, tiled=True)
    return pl.pallas_call(
        filter_kernel,
        out_shape=jax.ShapeDtypeStruct((128, 1024), F32),
        in_specs=[VMEM, VMEM],
        out_specs=VMEM,
        cost_estimate=pl.CostEstimate(flops=10**6, bytes_accessed=2 * 10**6, transcendentals=0),
        compiler_params=grant(8),
        name="filter",
    )(parts, keep)


def solution(mesh):
    spec = P("layer", "row", "col")
    out = P(("row", "layer"), "col")
    return jax.shard_map(
        body, mesh=mesh, in_specs=(spec, spec, spec, spec, out), out_specs=out, check_vma=False
    )
```

```python
import functools

import jax
import jax.numpy as jnp
from jax import lax
from jax.experimental import pallas as pl
from jax.experimental.pallas import tpu as pltpu
from jax.sharding import PartitionSpec as P

BS = 64
BR = 8
BC = 16
KB = 16
MOSTA = 2
MOSTB = 4
STEPS = 2
LAYERS = 4
NONE = 100
PIECE = 32
EXTRA = 8

F32, BF16, I32, I16 = jnp.float32, jnp.bfloat16, jnp.int32, jnp.int16
ANY = pl.BlockSpec(memory_space=pl.ANY)
VMEM = pl.BlockSpec(memory_space=pltpu.VMEM)


def grant(mib):
    return pltpu.CompilerParams(vmem_limit_bytes=mib * 2**20)


def lanes(rows=1):
    return lax.broadcasted_iota(I32, (rows, 128), 1)


def halves(left, right, rows=1):
    return jnp.where(lanes(rows) < BS, left, right)


def slot_ids(bits, most):
    ids = [jnp.int32(NONE)] * most
    seen = jnp.int32(0)
    for i, bit in enumerate(bits):
        one = bit != 0
        for s in range(most):
            ids[s] = jnp.where(one & (seen == s), jnp.int32(i), ids[s])
        seen = seen + one.astype(I32)
    return ids


def swap_halves(x):
    return jnp.concatenate([x[:, BS:], x[:, :BS]], axis=1)


def narrow(ids):
    return ids.astype(F32).astype(BF16)


def compact(panel, pairs, ids):
    outs = [jnp.zeros((BS, 128), BF16) for _ in range(len(ids) // 2)]
    wants = [narrow(halves(ids[2 * o], ids[2 * o + 1], BS)) for o in range(len(outs))]
    for p in range(pairs):
        straight = panel(p)
        turned = swap_halves(straight)
        here, there = (narrow(halves(*at, BS)) for at in ((2 * p, 2 * p + 1), (2 * p + 1, 2 * p)))
        for o in range(len(outs)):
            outs[o] = jnp.where(wants[o] == here, straight, outs[o])
            outs[o] = jnp.where(wants[o] == there, turned, outs[o])
    return outs


def pack_kernel(a_mask, b_mask, at, b, a_out, b_out, a_bits, b_bits, a_in, b_in, a_packed, b_packed, sems):
    loads = [
        pltpu.make_async_copy(source, target, sems.at[n])
        for n, (source, target) in enumerate(((b_mask, b_bits), (b, b_in), (a_mask, a_bits), (at, a_in)))
    ]
    for load in loads:
        load.start()
    row = lax.broadcasted_iota(I32, (EXTRA, 128), 0)

    loads[0].wait()
    ids = [slot_ids([b_bits[s, j] for j in range(BC)], MOSTB) for s in range(STEPS)]
    loads[1].wait()
    for s in range(STEPS):
        pair = compact(lambda p: b_in[s, :, 128 * p : 128 * p + 128], BC // 2, ids[s])
        for o in range(2):
            b_packed[BS * s : BS * s + BS, 128 * o : 128 * o + 128] = pair[o]
    for o in range(2):
        index = jnp.where(
            row == 0,
            halves(ids[0][2 * o], ids[0][2 * o + 1], EXTRA),
            halves(ids[1][2 * o], ids[1][2 * o + 1], EXTRA),
        )
        b_packed[128 : 128 + EXTRA, 128 * o : 128 * o + 128] = narrow(index)
    stores = [pltpu.make_async_copy(b_packed, b_out.at[d], sems.at[5 + d]) for d in range(KB)]
    for store in stores:
        store.start()

    loads[2].wait()
    ids = [slot_ids([a_bits[s, i] for i in range(BR)], MOSTA) for s in range(STEPS)]
    loads[3].wait()
    steps = [
        compact(lambda p: a_in[s, :, 128 * p : 128 * p + 128], BR // 2, ids[s])[0]
        for s in range(STEPS)
    ]
    a_packed[0:128, :] = jnp.concatenate(steps, axis=0).astype(F32).T.astype(BF16)
    index = jnp.where(
        row == 0,
        halves(ids[0][0], ids[1][0], EXTRA),
        halves(ids[0][1], ids[1][1], EXTRA),
    )
    a_packed[128 : 128 + EXTRA, :] = narrow(index)
    stores.append(pltpu.make_async_copy(a_packed, a_out, sems.at[4]))
    stores[-1].start()
    for store in stores:
        store.wait()


def turn(b, k, s):
    parts = []
    for o in range(2):
        index = b[k, 128 : 128 + EXTRA, 128 * o : 128 * o + 128].astype(F32)
        half = b[k, BS * s : BS * s + BS, 128 * o : 128 * o + 128]
        for ids, values in (
            (index, half),
            (swap_halves(index), jnp.concatenate([half[:, BS:], half[:, :BS]], axis=1)),
        ):
            parts.append((jnp.broadcast_to(ids[s : s + 1], (BS, 128)).astype(BF16), values))
    return parts


def pick(parts, p):
    target = halves(2 * p, 2 * p + 1, BS).astype(F32).astype(BF16)
    dense = jnp.zeros((BS, 128), BF16)
    for ids, values in parts:
        dense = jnp.where(ids == target, values, dense)
    return dense


def product_kernel(a, b, out):
    columns = []
    for c in range(KB):
        index = a[c, 128 : 128 + EXTRA, :].astype(F32)
        ids = [jnp.broadcast_to(index[s : s + 1], (BS, 128)).astype(BF16) for s in range(MOSTA)]
        blocks = []
        for i in range(BR):
            dense = jnp.zeros((BS, 128), BF16)
            for s in range(MOSTA):
                dense = jnp.where(ids[s] == jnp.bfloat16(i), a[c, BS * s : BS * s + BS, :], dense)
            blocks.append(dense)
        columns.append(jnp.concatenate(blocks, axis=0))
    left = jnp.concatenate(columns, axis=1)
    turned = {(k, s): turn(b, k, s) for k in range(KB) for s in range(STEPS)}
    rows = out.shape[1] - EXTRA
    tiles, width = 2, 512
    for t in range(tiles):
        cols = slice(width * t, width * t + width)
        dense = []
        for k in range(KB):
            for s in range(STEPS):
                parts = turned[k, s]
                dense.append(jnp.concatenate([pick(parts, 4 * t + h) for h in range(4)], axis=1))
        total = jnp.dot(left, jnp.concatenate(dense, axis=0), preferred_element_type=F32)
        for l in range(LAYERS):
            part = total[rows * l : rows * l + rows]
            top = jnp.max(jnp.abs(part), axis=0, keepdims=True)
            power = jnp.floor(jnp.log2(jnp.maximum(top, 1e-30))) - 13.0
            out[l, 0:rows, cols] = jnp.round(part * jnp.exp2(-power)).astype(I32).astype(I16)
            power = jnp.broadcast_to(power, (EXTRA, width))
            out[l, rows : rows + EXTRA, cols] = power.astype(I32).astype(I16)


def filter_kernel(parts, keep, out, total, sems):
    rows = out.shape[0]
    scales = [jnp.exp2(parts[l, rows : rows + EXTRA, :].astype(I32).astype(F32)[0:1]) for l in range(LAYERS)]
    stores = []
    for n, r in enumerate(range(0, rows, PIECE)):
        some = None
        for l in range(LAYERS):
            term = parts[l, r : r + PIECE, :].astype(I32).astype(F32) * scales[l]
            some = term if some is None else some + term
        total[r : r + PIECE, :] = some * keep[r // BS : r // BS + 1, :]
        here = pl.ds(r, PIECE)
        stores.append(pltpu.make_async_copy(total.at[here], out.at[here], sems.at[n]))
        stores[-1].start()
    for store in stores:
        store.wait()


def body(a_panel, b_panel, a_mask, b_mask, c_pattern):
    rows = 128 + EXTRA
    a_sent, b_sent = pl.pallas_call(
        pack_kernel,
        out_shape=(
            jax.ShapeDtypeStruct((rows, 128), BF16),
            jax.ShapeDtypeStruct((KB, rows, 256), BF16),
        ),
        in_specs=[ANY] * 4,
        out_specs=(ANY, ANY),
        scratch_shapes=[
            pltpu.SMEM((STEPS, BR), I32),
            pltpu.SMEM((STEPS, BC), I32),
            pltpu.VMEM((STEPS, BS, BR * BS), BF16),
            pltpu.VMEM((STEPS, BS, BC * BS), BF16),
            pltpu.VMEM((rows, 128), BF16),
            pltpu.VMEM((rows, 256), BF16),
            pltpu.SemaphoreType.DMA((5 + KB,)),
        ],
        cost_estimate=pl.CostEstimate(flops=10**6, bytes_accessed=2 * 10**6, transcendentals=0),
        name="pack",
    )(
        a_mask.reshape(STEPS, BR),
        b_mask.reshape(STEPS, BC),
        jnp.swapaxes(a_panel, 1, 2),
        b_panel,
    )
    b_all = lax.all_to_all(b_sent, "row", 0, 0, tiled=True)
    a_all = lax.all_gather(a_sent, "col")
    keep = jnp.repeat(c_pattern.astype(F32), BS, axis=1)
    sums = pl.pallas_call(
        product_kernel,
        out_shape=jax.ShapeDtypeStruct((LAYERS, 128 + EXTRA, 1024), I16),
        in_specs=[VMEM, VMEM],
        out_specs=VMEM,
        cost_estimate=pl.CostEstimate(flops=2 * 10**9, bytes_accessed=6 * 10**6, transcendentals=0),
        compiler_params=grant(24),
        name="product",
    )(a_all, b_all)
    parts = lax.all_to_all(sums, "layer", 0, 0, tiled=True)
    return pl.pallas_call(
        filter_kernel,
        out_shape=jax.ShapeDtypeStruct((128, 1024), F32),
        in_specs=[VMEM, VMEM],
        out_specs=ANY,
        scratch_shapes=[pltpu.VMEM((128, 1024), F32), pltpu.SemaphoreType.DMA((128 // PIECE,))],
        cost_estimate=pl.CostEstimate(flops=10**6, bytes_accessed=2 * 10**6, transcendentals=0),
        compiler_params=grant(8),
        name="filter",
    )(parts, keep)


def solution(mesh):
    spec = P("layer", "row", "col")
    out = P(("row", "layer"), "col")
    return jax.shard_map(
        body, mesh=mesh, in_specs=(spec, spec, spec, spec, out), out_specs=out, check_vma=False
    )
```

```python
import functools

import jax
import jax.numpy as jnp
from jax import lax
from jax.experimental import pallas as pl
from jax.experimental.pallas import tpu as pltpu
from jax.sharding import PartitionSpec as P

BS = 64
BR = 8
BC = 16
KB = 16
MOSTA = 2
MOSTB = 4
STEPS = 2
LAYERS = 4
NONE = 100
PIECE = 32
EXTRA = 8

F32, BF16, I32, I16 = jnp.float32, jnp.bfloat16, jnp.int32, jnp.int16
ANY = pl.BlockSpec(memory_space=pl.ANY)
VMEM = pl.BlockSpec(memory_space=pltpu.VMEM)


def grant(mib):
    return pltpu.CompilerParams(vmem_limit_bytes=mib * 2**20)


def lanes(rows=1):
    return lax.broadcasted_iota(I32, (rows, 128), 1)


def halves(left, right, rows=1):
    return jnp.where(lanes(rows) < BS, left, right)


def slot_ids(bits, most):
    ids = [jnp.int32(NONE)] * most
    seen = jnp.int32(0)
    for i, bit in enumerate(bits):
        one = bit != 0
        for s in range(most):
            ids[s] = jnp.where(one & (seen == s), jnp.int32(i), ids[s])
        seen = seen + one.astype(I32)
    return ids


def swap_halves(x):
    return jnp.concatenate([x[:, BS:], x[:, :BS]], axis=1)


def narrow(ids):
    return ids.astype(F32).astype(BF16)


def compact(panel, pairs, ids):
    outs = [jnp.zeros((BS, 128), BF16) for _ in range(len(ids) // 2)]
    wants = [narrow(halves(ids[2 * o], ids[2 * o + 1], BS)) for o in range(len(outs))]
    for p in range(pairs):
        straight = panel(p)
        turned = swap_halves(straight)
        here, there = (narrow(halves(*at, BS)) for at in ((2 * p, 2 * p + 1), (2 * p + 1, 2 * p)))
        for o in range(len(outs)):
            outs[o] = jnp.where(wants[o] == here, straight, outs[o])
            outs[o] = jnp.where(wants[o] == there, turned, outs[o])
    return outs


def pack_kernel(a_mask, b_mask, at, b, a_out, b_out, a_bits, b_bits, a_in, b_in, a_packed, b_packed, sems):
    pairs = (
        (b_mask, b_bits),
        (b.at[0], b_in.at[0]),
        (a_mask, a_bits),
        (at, a_in),
        (b.at[1], b_in.at[1]),
    )
    loads = [
        pltpu.make_async_copy(source, target, sems.at[n])
        for n, (source, target) in enumerate(pairs)
    ]
    for n in (0, 1, 4, 2, 3):
        loads[n].start()
    row = lax.broadcasted_iota(I32, (EXTRA, 128), 0)

    loads[0].wait()
    ids = [slot_ids([b_bits[s, j] for j in range(BC)], MOSTB) for s in range(STEPS)]
    for o in range(2):
        index = jnp.where(
            row == 0,
            halves(ids[0][2 * o], ids[0][2 * o + 1], EXTRA),
            halves(ids[1][2 * o], ids[1][2 * o + 1], EXTRA),
        )
        b_packed[128 : 128 + EXTRA, 128 * o : 128 * o + 128] = narrow(index)
    stores = []
    for s in range(STEPS):
        loads[(1, 4)[s]].wait()
        pair = compact(lambda p: b_in[s, :, 128 * p : 128 * p + 128], BC // 2, ids[s])
        for o in range(2):
            b_packed[BS * s : BS * s + BS, 128 * o : 128 * o + 128] = pair[o]
        here = pl.ds(BS * s, BS + EXTRA * s)
        for d in range(KB):
            sem = sems.at[6 + KB * s + d]
            stores.append(pltpu.make_async_copy(b_packed.at[here], b_out.at[d, here], sem))
            stores[-1].start()

    loads[2].wait()
    ids = [slot_ids([a_bits[s, i] for i in range(BR)], MOSTA) for s in range(STEPS)]
    loads[3].wait()
    steps = [
        compact(lambda p: a_in[s, :, 128 * p : 128 * p + 128], BR // 2, ids[s])[0]
        for s in range(STEPS)
    ]
    a_packed[0:128, :] = jnp.concatenate(steps, axis=0).astype(F32).T.astype(BF16)
    index = jnp.where(
        row == 0,
        halves(ids[0][0], ids[1][0], EXTRA),
        halves(ids[0][1], ids[1][1], EXTRA),
    )
    a_packed[128 : 128 + EXTRA, :] = narrow(index)
    stores.append(pltpu.make_async_copy(a_packed, a_out, sems.at[5]))
    stores[-1].start()
    for store in stores:
        store.wait()


def turn(b, k, s):
    parts = []
    for o in range(2):
        index = b[k, 128 : 128 + EXTRA, 128 * o : 128 * o + 128].astype(F32)
        half = b[k, BS * s : BS * s + BS, 128 * o : 128 * o + 128]
        for ids, values in (
            (index, half),
            (swap_halves(index), jnp.concatenate([half[:, BS:], half[:, :BS]], axis=1)),
        ):
            parts.append((jnp.broadcast_to(ids[s : s + 1], (BS, 128)).astype(BF16), values))
    return parts


def pick(parts, p):
    target = halves(2 * p, 2 * p + 1, BS).astype(F32).astype(BF16)
    dense = jnp.zeros((BS, 128), BF16)
    for ids, values in parts:
        dense = jnp.where(ids == target, values, dense)
    return dense


def product_kernel(a, b, out):
    columns = []
    for c in range(KB):
        index = a[128 : 128 + EXTRA, 128 * c : 128 * c + 128].astype(F32)
        ids = [jnp.broadcast_to(index[s : s + 1], (BS, 128)).astype(BF16) for s in range(MOSTA)]
        blocks = []
        for i in range(BR):
            dense = jnp.zeros((BS, 128), BF16)
            for s in range(MOSTA):
                dense = jnp.where(ids[s] == jnp.bfloat16(i), a[BS * s : BS * s + BS, 128 * c : 128 * c + 128], dense)
            blocks.append(dense)
        columns.append(jnp.concatenate(blocks, axis=0))
    left = jnp.concatenate(columns, axis=1)
    turned = {(k, s): turn(b, k, s) for k in range(KB) for s in range(STEPS)}
    rows = out.shape[1] - EXTRA
    tiles, width = 2, 512
    for t in range(tiles):
        cols = slice(width * t, width * t + width)
        dense = []
        for k in range(KB):
            for s in range(STEPS):
                parts = turned[k, s]
                dense.append(jnp.concatenate([pick(parts, 4 * t + h) for h in range(4)], axis=1))
        total = jnp.dot(left, jnp.concatenate(dense, axis=0), preferred_element_type=F32)
        for l in range(LAYERS):
            part = total[rows * l : rows * l + rows]
            top = jnp.max(jnp.abs(part), axis=0, keepdims=True)
            power = jnp.floor(jnp.log2(jnp.maximum(top, 1e-30))) - 13.0
            out[l, 0:rows, cols] = jnp.round(part * jnp.exp2(-power)).astype(I32).astype(I16)
            power = jnp.broadcast_to(power, (EXTRA, width))
            out[l, rows : rows + EXTRA, cols] = power.astype(I32).astype(I16)


def filter_kernel(parts, keep, out, total, sems):
    rows = out.shape[0]
    scales = [jnp.exp2(parts[l, rows : rows + EXTRA, :].astype(I32).astype(F32)[0:1]) for l in range(LAYERS)]
    stores = []
    for n, r in enumerate(range(0, rows, PIECE)):
        some = None
        for l in range(LAYERS):
            term = parts[l, r : r + PIECE, :].astype(I32).astype(F32) * scales[l]
            some = term if some is None else some + term
        total[r : r + PIECE, :] = some * keep[r // BS : r // BS + 1, :]
        here = pl.ds(r, PIECE)
        stores.append(pltpu.make_async_copy(total.at[here], out.at[here], sems.at[n]))
        stores[-1].start()
    for store in stores:
        store.wait()


def body(a_panel, b_panel, a_mask, b_mask, c_pattern):
    rows = 128 + EXTRA
    a_sent, b_sent = pl.pallas_call(
        pack_kernel,
        out_shape=(
            jax.ShapeDtypeStruct((rows, 128), BF16),
            jax.ShapeDtypeStruct((KB, rows, 256), BF16),
        ),
        in_specs=[ANY] * 4,
        out_specs=(ANY, ANY),
        scratch_shapes=[
            pltpu.SMEM((STEPS, BR), I32),
            pltpu.SMEM((STEPS, BC), I32),
            pltpu.VMEM((STEPS, BS, BR * BS), BF16),
            pltpu.VMEM((STEPS, BS, BC * BS), BF16),
            pltpu.VMEM((rows, 128), BF16),
            pltpu.VMEM((rows, 256), BF16),
            pltpu.SemaphoreType.DMA((6 + STEPS * KB,)),
        ],
        cost_estimate=pl.CostEstimate(flops=10**6, bytes_accessed=2 * 10**6, transcendentals=0),
        name="pack",
    )(
        a_mask.reshape(STEPS, BR),
        b_mask.reshape(STEPS, BC),
        jnp.swapaxes(a_panel, 1, 2),
        b_panel,
    )
    b_all = lax.all_to_all(b_sent, "row", 0, 0, tiled=True)
    a_all = lax.all_gather(a_sent, "col", axis=1, tiled=True)
    keep = jnp.repeat(c_pattern.astype(F32), BS, axis=1)
    sums = pl.pallas_call(
        product_kernel,
        out_shape=jax.ShapeDtypeStruct((LAYERS, 128 + EXTRA, 1024), I16),
        in_specs=[VMEM, VMEM],
        out_specs=VMEM,
        cost_estimate=pl.CostEstimate(flops=2 * 10**9, bytes_accessed=6 * 10**6, transcendentals=0),
        compiler_params=grant(24),
        name="product",
    )(a_all, b_all)
    parts = lax.all_to_all(sums, "layer", 0, 0, tiled=True)
    return pl.pallas_call(
        filter_kernel,
        out_shape=jax.ShapeDtypeStruct((128, 1024), F32),
        in_specs=[VMEM, VMEM],
        out_specs=ANY,
        scratch_shapes=[pltpu.VMEM((128, 1024), F32), pltpu.SemaphoreType.DMA((128 // PIECE,))],
        cost_estimate=pl.CostEstimate(flops=10**6, bytes_accessed=2 * 10**6, transcendentals=0),
        compiler_params=grant(8),
        name="filter",
    )(parts, keep)


def solution(mesh):
    spec = P("layer", "row", "col")
    out = P(("row", "layer"), "col")
    return jax.shard_map(
        body, mesh=mesh, in_specs=(spec, spec, spec, spec, out), out_specs=out, check_vma=False
    )
```

```python
import functools

import jax
import jax.numpy as jnp
from jax import lax
from jax.experimental import pallas as pl
from jax.experimental.pallas import tpu as pltpu
from jax.sharding import PartitionSpec as P

BS = 64
BR = 8
BC = 16
KB = 16
MOSTA = 2
MOSTB = 4
STEPS = 2
LAYERS = 4
NONE = 100
PIECE = 32
EXTRA = 8

F32, BF16, I32, I16 = jnp.float32, jnp.bfloat16, jnp.int32, jnp.int16
ANY = pl.BlockSpec(memory_space=pl.ANY)
VMEM = pl.BlockSpec(memory_space=pltpu.VMEM)


def grant(mib):
    return pltpu.CompilerParams(vmem_limit_bytes=mib * 2**20)


def lanes(rows=1):
    return lax.broadcasted_iota(I32, (rows, 128), 1)


def halves(left, right, rows=1):
    return jnp.where(lanes(rows) < BS, left, right)


def slot_ids(bits, most):
    ids = [jnp.int32(NONE)] * most
    seen = jnp.int32(0)
    for i, bit in enumerate(bits):
        one = bit != 0
        for s in range(most):
            ids[s] = jnp.where(one & (seen == s), jnp.int32(i), ids[s])
        seen = seen + one.astype(I32)
    return ids


def swap_halves(x):
    return jnp.concatenate([x[:, BS:], x[:, :BS]], axis=1)


def narrow(ids):
    return ids.astype(F32).astype(BF16)


def compact(panel, pairs, ids):
    outs = [jnp.zeros((BS, 128), BF16) for _ in range(len(ids) // 2)]
    wants = [narrow(halves(ids[2 * o], ids[2 * o + 1], BS)) for o in range(len(outs))]
    for p in range(pairs):
        straight = panel(p)
        turned = swap_halves(straight)
        here, there = (narrow(halves(*at, BS)) for at in ((2 * p, 2 * p + 1), (2 * p + 1, 2 * p)))
        for o in range(len(outs)):
            outs[o] = jnp.where(wants[o] == here, straight, outs[o])
            outs[o] = jnp.where(wants[o] == there, turned, outs[o])
    return outs


def pack_kernel(a_mask, b_mask, at, b, a_out, b_out, a_bits, b_bits, a_in, b_in, a_packed, b_packed, sems):
    loads = [
        pltpu.make_async_copy(source, target, sems.at[n])
        for n, (source, target) in enumerate(((b_mask, b_bits), (b, b_in), (a_mask, a_bits), (at, a_in)))
    ]
    for load in loads:
        load.start()
    row = lax.broadcasted_iota(I32, (EXTRA, 128), 0)

    loads[0].wait()
    ids = [slot_ids([b_bits[s, j] for j in range(BC)], MOSTB) for s in range(STEPS)]
    loads[1].wait()
    for s in range(STEPS):
        pair = compact(lambda p: b_in[s, :, 128 * p : 128 * p + 128], BC // 2, ids[s])
        for o in range(2):
            b_packed[BS * s : BS * s + BS, 128 * o : 128 * o + 128] = pair[o]
    for o in range(2):
        index = jnp.where(
            row == 0,
            halves(ids[0][2 * o], ids[0][2 * o + 1], EXTRA),
            halves(ids[1][2 * o], ids[1][2 * o + 1], EXTRA),
        )
        b_packed[128 : 128 + EXTRA, 128 * o : 128 * o + 128] = narrow(index)
    stores = [pltpu.make_async_copy(b_packed, b_out.at[d], sems.at[5 + d]) for d in range(KB)]
    for store in stores:
        store.start()

    loads[2].wait()
    ids = [slot_ids([a_bits[s, i] for i in range(BR)], MOSTA) for s in range(STEPS)]
    loads[3].wait()
    steps = [
        compact(lambda p: a_in[s, :, 128 * p : 128 * p + 128], BR // 2, ids[s])[0]
        for s in range(STEPS)
    ]
    a_packed[0:128, :] = jnp.concatenate(steps, axis=0).astype(F32).T.astype(BF16)
    index = jnp.where(
        row == 0,
        halves(ids[0][0], ids[1][0], EXTRA),
        halves(ids[0][1], ids[1][1], EXTRA),
    )
    a_packed[128 : 128 + EXTRA, :] = narrow(index)
    stores.append(pltpu.make_async_copy(a_packed, a_out, sems.at[4]))
    stores[-1].start()
    for store in stores:
        store.wait()


def turn(b, k, s):
    parts = []
    for o in range(2):
        index = b[k, 128 : 128 + EXTRA, 128 * o : 128 * o + 128].astype(F32)
        half = b[k, BS * s : BS * s + BS, 128 * o : 128 * o + 128]
        for ids, values in (
            (index, half),
            (swap_halves(index), jnp.concatenate([half[:, BS:], half[:, :BS]], axis=1)),
        ):
            parts.append((jnp.broadcast_to(ids[s : s + 1], (BS, 128)).astype(BF16), values))
    return parts


def pick(parts, p):
    target = halves(2 * p, 2 * p + 1, BS).astype(F32).astype(BF16)
    dense = jnp.zeros((BS, 128), BF16)
    for ids, values in parts:
        dense = jnp.where(ids == target, values, dense)
    return dense


def product_kernel(a, b, sent, out, sems):
    columns = []
    for c in range(KB):
        index = a[c, 128 : 128 + EXTRA, :].astype(F32)
        ids = [jnp.broadcast_to(index[s : s + 1], (BS, 128)).astype(BF16) for s in range(MOSTA)]
        blocks = []
        for i in range(BR):
            dense = jnp.zeros((BS, 128), BF16)
            for s in range(MOSTA):
                dense = jnp.where(ids[s] == jnp.bfloat16(i), a[c, BS * s : BS * s + BS, :], dense)
            blocks.append(dense)
        columns.append(jnp.concatenate(blocks, axis=0))
    left = jnp.concatenate(columns, axis=1)
    turned = {(k, s): turn(b, k, s) for k in range(KB) for s in range(STEPS)}
    rows = out.shape[1] - EXTRA
    tiles, width = 2, 512
    stores = []
    for t in range(tiles):
        cols = slice(width * t, width * t + width)
        dense = []
        for k in range(KB):
            for s in range(STEPS):
                parts = turned[k, s]
                dense.append(jnp.concatenate([pick(parts, 4 * t + h) for h in range(4)], axis=1))
        total = jnp.dot(left, jnp.concatenate(dense, axis=0), preferred_element_type=F32)
        for l in range(LAYERS):
            part = total[rows * l : rows * l + rows]
            top = jnp.max(jnp.abs(part), axis=0, keepdims=True)
            power = jnp.floor(jnp.log2(jnp.maximum(top, 1e-30))) - 13.0
            out[l, 0:rows, cols] = jnp.round(part * jnp.exp2(-power)).astype(I32).astype(I16)
            power = jnp.broadcast_to(power, (EXTRA, width))
            out[l, rows : rows + EXTRA, cols] = power.astype(I32).astype(I16)
        here = pl.ds(width * t, width)
        stores.append(pltpu.make_async_copy(out.at[:, :, here], sent.at[:, :, here], sems.at[t]))
        stores[-1].start()
    for store in stores:
        store.wait()


def filter_kernel(parts, keep, out, total, sems):
    rows = out.shape[0]
    scales = [jnp.exp2(parts[l, rows : rows + EXTRA, :].astype(I32).astype(F32)[0:1]) for l in range(LAYERS)]
    stores = []
    for n, r in enumerate(range(0, rows, PIECE)):
        some = None
        for l in range(LAYERS):
            term = parts[l, r : r + PIECE, :].astype(I32).astype(F32) * scales[l]
            some = term if some is None else some + term
        total[r : r + PIECE, :] = some * keep[r // BS : r // BS + 1, :]
        here = pl.ds(r, PIECE)
        stores.append(pltpu.make_async_copy(total.at[here], out.at[here], sems.at[n]))
        stores[-1].start()
    for store in stores:
        store.wait()


def body(a_panel, b_panel, a_mask, b_mask, c_pattern):
    rows = 128 + EXTRA
    a_sent, b_sent = pl.pallas_call(
        pack_kernel,
        out_shape=(
            jax.ShapeDtypeStruct((rows, 128), BF16),
            jax.ShapeDtypeStruct((KB, rows, 256), BF16),
        ),
        in_specs=[ANY] * 4,
        out_specs=(ANY, ANY),
        scratch_shapes=[
            pltpu.SMEM((STEPS, BR), I32),
            pltpu.SMEM((STEPS, BC), I32),
            pltpu.VMEM((STEPS, BS, BR * BS), BF16),
            pltpu.VMEM((STEPS, BS, BC * BS), BF16),
            pltpu.VMEM((rows, 128), BF16),
            pltpu.VMEM((rows, 256), BF16),
            pltpu.SemaphoreType.DMA((5 + KB,)),
        ],
        cost_estimate=pl.CostEstimate(flops=10**6, bytes_accessed=2 * 10**6, transcendentals=0),
        name="pack",
    )(
        a_mask.reshape(STEPS, BR),
        b_mask.reshape(STEPS, BC),
        jnp.swapaxes(a_panel, 1, 2),
        b_panel,
    )
    b_all = lax.all_to_all(b_sent, "row", 0, 0, tiled=True)
    a_all = lax.all_gather(a_sent, "col")
    keep = jnp.repeat(c_pattern.astype(F32), BS, axis=1)
    sums = pl.pallas_call(
        product_kernel,
        out_shape=jax.ShapeDtypeStruct((LAYERS, 128 + EXTRA, 1024), I16),
        in_specs=[VMEM, VMEM],
        out_specs=ANY,
        scratch_shapes=[
            pltpu.VMEM((LAYERS, 128 + EXTRA, 1024), I16),
            pltpu.SemaphoreType.DMA((2,)),
        ],
        cost_estimate=pl.CostEstimate(flops=2 * 10**9, bytes_accessed=6 * 10**6, transcendentals=0),
        compiler_params=grant(24),
        name="product",
    )(a_all, b_all)
    parts = lax.all_to_all(sums, "layer", 0, 0, tiled=True)
    return pl.pallas_call(
        filter_kernel,
        out_shape=jax.ShapeDtypeStruct((128, 1024), F32),
        in_specs=[VMEM, VMEM],
        out_specs=ANY,
        scratch_shapes=[pltpu.VMEM((128, 1024), F32), pltpu.SemaphoreType.DMA((128 // PIECE,))],
        cost_estimate=pl.CostEstimate(flops=10**6, bytes_accessed=2 * 10**6, transcendentals=0),
        compiler_params=grant(8),
        name="filter",
    )(parts, keep)


def solution(mesh):
    spec = P("layer", "row", "col")
    out = P(("row", "layer"), "col")
    return jax.shard_map(
        body, mesh=mesh, in_specs=(spec, spec, spec, spec, out), out_specs=out, check_vma=False
    )
```

```python
import functools

import jax
import jax.numpy as jnp
from jax import lax
from jax.experimental import pallas as pl
from jax.experimental.pallas import tpu as pltpu
from jax.sharding import PartitionSpec as P

BS = 64
BR = 8
BC = 16
KB = 16
MOSTA = 2
MOSTB = 4
STEPS = 2
LAYERS = 4
NONE = 100
PIECE = 32
EXTRA = 8

F32, BF16, I32, I16 = jnp.float32, jnp.bfloat16, jnp.int32, jnp.int16
ANY = pl.BlockSpec(memory_space=pl.ANY)
VMEM = pl.BlockSpec(memory_space=pltpu.VMEM)


def grant(mib):
    return pltpu.CompilerParams(vmem_limit_bytes=mib * 2**20)


def lanes(rows=1):
    return lax.broadcasted_iota(I32, (rows, 128), 1)


def halves(left, right, rows=1):
    return jnp.where(lanes(rows) < BS, left, right)


def slot_ids(bits, most):
    ids = [jnp.int32(NONE)] * most
    seen = jnp.int32(0)
    for i, bit in enumerate(bits):
        one = bit != 0
        for s in range(most):
            ids[s] = jnp.where(one & (seen == s), jnp.int32(i), ids[s])
        seen = seen + one.astype(I32)
    return ids


def swap_halves(x):
    return jnp.concatenate([x[:, BS:], x[:, :BS]], axis=1)


def narrow(ids):
    return ids.astype(F32).astype(BF16)


def compact(panel, pairs, ids):
    outs = [jnp.zeros((BS, 128), BF16) for _ in range(len(ids) // 2)]
    wants = [narrow(halves(ids[2 * o], ids[2 * o + 1], BS)) for o in range(len(outs))]
    for p in range(pairs):
        straight = panel(p)
        turned = swap_halves(straight)
        here, there = (narrow(halves(*at, BS)) for at in ((2 * p, 2 * p + 1), (2 * p + 1, 2 * p)))
        for o in range(len(outs)):
            outs[o] = jnp.where(wants[o] == here, straight, outs[o])
            outs[o] = jnp.where(wants[o] == there, turned, outs[o])
    return outs


def pack_kernel(a_mask, b_mask, at, b, a_out, b_out, a_bits, b_bits, a_in, b_in, a_packed, b_packed, sems):
    pairs = (
        (b_mask, b_bits),
        (b.at[0], b_in.at[0]),
        (a_mask, a_bits),
        (at, a_in),
        (b.at[1], b_in.at[1]),
    )
    loads = [
        pltpu.make_async_copy(source, target, sems.at[n])
        for n, (source, target) in enumerate(pairs)
    ]
    for n in (0, 1, 4, 2, 3):
        loads[n].start()
    row = lax.broadcasted_iota(I32, (EXTRA, 128), 0)

    loads[0].wait()
    ids = [slot_ids([b_bits[s, j] for j in range(BC)], MOSTB) for s in range(STEPS)]
    for o in range(2):
        index = jnp.where(
            row == 0,
            halves(ids[0][2 * o], ids[0][2 * o + 1], EXTRA),
            halves(ids[1][2 * o], ids[1][2 * o + 1], EXTRA),
        )
        b_packed[128 : 128 + EXTRA, 128 * o : 128 * o + 128] = narrow(index)
    stores = []
    for s in range(STEPS):
        loads[(1, 4)[s]].wait()
        pair = compact(lambda p: b_in[s, :, 128 * p : 128 * p + 128], BC // 2, ids[s])
        for o in range(2):
            b_packed[BS * s : BS * s + BS, 128 * o : 128 * o + 128] = pair[o]
        here = pl.ds(BS * s, BS + EXTRA * s)
        for d in range(KB):
            sem = sems.at[6 + KB * s + d]
            stores.append(pltpu.make_async_copy(b_packed.at[here], b_out.at[d, here], sem))
            stores[-1].start()

    loads[2].wait()
    ids = [slot_ids([a_bits[s, i] for i in range(BR)], MOSTA) for s in range(STEPS)]
    loads[3].wait()
    steps = [
        compact(lambda p: a_in[s, :, 128 * p : 128 * p + 128], BR // 2, ids[s])[0]
        for s in range(STEPS)
    ]
    a_packed[0:128, :] = jnp.concatenate(steps, axis=0).astype(F32).T.astype(BF16)
    index = jnp.where(
        row == 0,
        halves(ids[0][0], ids[1][0], EXTRA),
        halves(ids[0][1], ids[1][1], EXTRA),
    )
    a_packed[128 : 128 + EXTRA, :] = narrow(index)
    stores.append(pltpu.make_async_copy(a_packed, a_out, sems.at[5]))
    stores[-1].start()
    for store in stores:
        store.wait()


def turn(b, k, s):
    parts = []
    for o in range(2):
        index = b[k, 128 : 128 + EXTRA, 128 * o : 128 * o + 128].astype(F32)
        half = b[k, BS * s : BS * s + BS, 128 * o : 128 * o + 128]
        for ids, values in (
            (index, half),
            (swap_halves(index), jnp.concatenate([half[:, BS:], half[:, :BS]], axis=1)),
        ):
            parts.append((jnp.broadcast_to(ids[s : s + 1], (BS, 128)).astype(BF16), values))
    return parts


def pick(parts, p):
    target = halves(2 * p, 2 * p + 1, BS).astype(F32).astype(BF16)
    dense = jnp.zeros((BS, 128), BF16)
    for ids, values in parts:
        dense = jnp.where(ids == target, values, dense)
    return dense


def product_kernel(a, b, sent, out, sems):
    columns = []
    for c in range(KB):
        index = a[c, 128 : 128 + EXTRA, :].astype(F32)
        ids = [jnp.broadcast_to(index[s : s + 1], (BS, 128)).astype(BF16) for s in range(MOSTA)]
        blocks = []
        for i in range(BR):
            dense = jnp.zeros((BS, 128), BF16)
            for s in range(MOSTA):
                dense = jnp.where(ids[s] == jnp.bfloat16(i), a[c, BS * s : BS * s + BS, :], dense)
            blocks.append(dense)
        columns.append(jnp.concatenate(blocks, axis=0))
    left = jnp.concatenate(columns, axis=1)
    turned = {(k, s): turn(b, k, s) for k in range(KB) for s in range(STEPS)}
    rows = out.shape[1] - EXTRA
    tiles, width = 2, 512
    stores = []
    for t in range(tiles):
        cols = slice(width * t, width * t + width)
        dense = []
        for k in range(KB):
            for s in range(STEPS):
                parts = turned[k, s]
                dense.append(jnp.concatenate([pick(parts, 4 * t + h) for h in range(4)], axis=1))
        total = jnp.dot(left, jnp.concatenate(dense, axis=0), preferred_element_type=F32)
        for l in range(LAYERS):
            part = total[rows * l : rows * l + rows]
            top = jnp.max(jnp.abs(part), axis=0, keepdims=True)
            power = jnp.floor(jnp.log2(jnp.maximum(top, 1e-30))) - 13.0
            out[l, 0:rows, cols] = jnp.round(part * jnp.exp2(-power)).astype(I32).astype(I16)
            power = jnp.broadcast_to(power, (EXTRA, width))
            out[l, rows : rows + EXTRA, cols] = power.astype(I32).astype(I16)
        here = pl.ds(width * t, width)
        stores.append(pltpu.make_async_copy(out.at[:, :, here], sent.at[:, :, here], sems.at[t]))
        stores[-1].start()
    for store in stores:
        store.wait()


def filter_kernel(parts, keep, out, total, sems):
    rows = out.shape[0]
    scales = [jnp.exp2(parts[l, rows : rows + EXTRA, :].astype(I32).astype(F32)[0:1]) for l in range(LAYERS)]
    stores = []
    for n, r in enumerate(range(0, rows, PIECE)):
        some = None
        for l in range(LAYERS):
            term = parts[l, r : r + PIECE, :].astype(I32).astype(F32) * scales[l]
            some = term if some is None else some + term
        total[r : r + PIECE, :] = some * keep[r // BS : r // BS + 1, :]
        here = pl.ds(r, PIECE)
        stores.append(pltpu.make_async_copy(total.at[here], out.at[here], sems.at[n]))
        stores[-1].start()
    for store in stores:
        store.wait()


def body(a_panel, b_panel, a_mask, b_mask, c_pattern):
    rows = 128 + EXTRA
    a_sent, b_sent = pl.pallas_call(
        pack_kernel,
        out_shape=(
            jax.ShapeDtypeStruct((rows, 128), BF16),
            jax.ShapeDtypeStruct((KB, rows, 256), BF16),
        ),
        in_specs=[ANY] * 4,
        out_specs=(ANY, ANY),
        scratch_shapes=[
            pltpu.SMEM((STEPS, BR), I32),
            pltpu.SMEM((STEPS, BC), I32),
            pltpu.VMEM((STEPS, BS, BR * BS), BF16),
            pltpu.VMEM((STEPS, BS, BC * BS), BF16),
            pltpu.VMEM((rows, 128), BF16),
            pltpu.VMEM((rows, 256), BF16),
            pltpu.SemaphoreType.DMA((6 + STEPS * KB,)),
        ],
        cost_estimate=pl.CostEstimate(flops=10**6, bytes_accessed=2 * 10**6, transcendentals=0),
        name="pack",
    )(
        a_mask.reshape(STEPS, BR),
        b_mask.reshape(STEPS, BC),
        jnp.swapaxes(a_panel, 1, 2),
        b_panel,
    )
    b_all = lax.all_to_all(b_sent, "row", 0, 0, tiled=True)
    a_all = lax.all_gather(a_sent, "col")
    keep = jnp.repeat(c_pattern.astype(F32), BS, axis=1)
    sums = pl.pallas_call(
        product_kernel,
        out_shape=jax.ShapeDtypeStruct((LAYERS, 128 + EXTRA, 1024), I16),
        in_specs=[VMEM, VMEM],
        out_specs=ANY,
        scratch_shapes=[
            pltpu.VMEM((LAYERS, 128 + EXTRA, 1024), I16),
            pltpu.SemaphoreType.DMA((2,)),
        ],
        cost_estimate=pl.CostEstimate(flops=2 * 10**9, bytes_accessed=6 * 10**6, transcendentals=0),
        compiler_params=grant(24),
        name="product",
    )(a_all, b_all)
    parts = lax.all_to_all(sums, "layer", 0, 0, tiled=True)
    return pl.pallas_call(
        filter_kernel,
        out_shape=jax.ShapeDtypeStruct((128, 1024), F32),
        in_specs=[VMEM, VMEM],
        out_specs=ANY,
        scratch_shapes=[pltpu.VMEM((128, 1024), F32), pltpu.SemaphoreType.DMA((128 // PIECE,))],
        cost_estimate=pl.CostEstimate(flops=10**6, bytes_accessed=2 * 10**6, transcendentals=0),
        compiler_params=grant(8),
        name="filter",
    )(parts, keep)


def solution(mesh):
    spec = P("layer", "row", "col")
    out = P(("row", "layer"), "col")
    return jax.shard_map(
        body, mesh=mesh, in_specs=(spec, spec, spec, spec, out), out_specs=out, check_vma=False
    )
```
